32 devices in a mesh: space: 2 (over y), energy: 16 (over z, x, core).
Axes of the slice: x: 2, y: 2, z: 4, core: 2. Of those that a mesh axis runs over, the one named last changes fastest.
Arguments:
- green_lesser: bfloat16 [16, 2, 2, 256, 256], P('energy', 'space'), may hold values from -6 to 6
- screened_lesser: bfloat16 [16, 2, 2, 256, 256], P('energy', 'space'), may hold values from -1.5 to 1.5
- green_retarded: bfloat16 [16, 2, 2, 256, 256], P('energy', 'space'), may hold values from -6 to 6
- screened_retarded: bfloat16 [16, 2, 2, 256, 256], P('energy', 'space'), may hold values from -1.5 to 1.5
- left_green: bfloat16 [16, 2, 2, 256, 256], P('energy', 'space'), may hold values from -0.25 to 0.25
- coupling: bfloat16 [2, 2, 256, 256], P('space'), may hold values from -0.25 to 0.25
Outputs:
- lesser_left: bfloat16 [16, 2, 2, 256, 256], P('energy', 'space')
- sigma_retarded: bfloat16 [16, 2, 2, 256, 256], P('energy', 'space')
The draws below stay inside these ranges and needn't reach their ends.
All inputs are finite; a program needn't handle non-finite values.
Results may differ from the reference program's by a relative error of at most 0.018.
Values may be sent and summed in bfloat16 or wider, within the bound.
No kernel may reach another device: no remote copies, remote signals or barrier semaphores. Data moves between devices by JAX's collectives and lax.ppermute only.
A program may use at most 64 MiB of HBM per device.

```python
import jax
import jax.numpy as jnp
from jax import lax

B = 256
NE = 16
NSLAB = 2


def steps_of(rng, dims, pieces, low, largest):
    def one(position, parts):
        draws = jax.random.uniform(jax.random.fold_in(jax.random.fold_in(rng, 6), position), (parts,), jnp.float32, low / len(pieces), largest / len(pieces))
        return jnp.repeat(jnp.exp(draws), dims[position] // parts).reshape((-1,) + (1,) * (len(dims) - position - 1))

    factor_of = one(*pieces[0])
    for cut in pieces[1:]:
        factor_of = factor_of * one(*cut)
    return factor_of


def gaussian(key, shape, scale, reach, pieces=(), kind=jnp.bfloat16):
    values = jax.random.normal(key, shape, jnp.float32) * scale
    if len(pieces) > 0:
        values = steps_of(key, shape, pieces, -0.22, 0.18) * values
    return jnp.clip(values, min=-reach, max=reach).astype(kind)


def setup_inputs(seed: int = 0) -> dict:
    key_list = jax.random.split(jax.random.key(seed), 7)
    return {
        "green_lesser": gaussian(key_list[0], (NE, NSLAB, 2, B, B), 1.0, 6.0, ((0, 16), (1, 2))),
        "screened_lesser": gaussian(key_list[1], (NE, NSLAB, 2, B, B), NE ** -0.5, 1.5, ((0, 16), (1, 2))),
        "green_retarded": gaussian(key_list[2], (NE, NSLAB, 2, B, B), 1.0, 6.0, ((0, 16), (1, 2))),
        "screened_retarded": gaussian(key_list[3], (NE, NSLAB, 2, B, B), NE ** -0.5, 1.5, ((0, 16), (1, 2))),
        "left_green": gaussian(key_list[4], (NE, NSLAB, 2, B, B), (2 * B) ** -0.5, 0.25, ((0, 16), (1, 2))),
        "coupling": gaussian(key_list[5], (NSLAB, 2, B, B), (2 * B) ** -0.5, 0.25, ((0, 2),)),
    }


def contract(einsum_pattern, first_factor, second_factor):
    return jnp.einsum(einsum_pattern, first_factor, second_factor, precision=lax.Precision.HIGHEST, preferred_element_type=jnp.float32)


def complex_product(einsum_pattern, first_factor, second_factor):
    first_real, first_imag = first_factor[..., 0, :, :], first_factor[..., 1, :, :]
    second_real, second_imag = second_factor[..., 0, :, :], second_factor[..., 1, :, :]
    real_part = contract(einsum_pattern, first_real, second_real) - contract(einsum_pattern, first_imag, second_imag)
    imag_part = contract(einsum_pattern, first_real, second_imag) + contract(einsum_pattern, first_imag, second_real)
    return jnp.stack([real_part, imag_part], axis=-3)


def adjoint_product(einsum_pattern, first_factor, second_factor):
    first_real, first_imag = first_factor[..., 0, :, :], first_factor[..., 1, :, :]
    second_real, second_imag = second_factor[..., 0, :, :], second_factor[..., 1, :, :]
    real_part = contract(einsum_pattern, first_real, second_real) + contract(einsum_pattern, first_imag, second_imag)
    imag_part = contract(einsum_pattern, first_imag, second_real) - contract(einsum_pattern, first_real, second_imag)
    return jnp.stack([real_part, imag_part], axis=-3)


def rounded(values):
    return lax.optimization_barrier(values.astype(jnp.bfloat16))


def as_complex(stacked):
    values = stacked.astype(jnp.float32)
    return values[:, 0] + 1j * values[:, 1]


def spectrum_green(stacked):
    values = as_complex(stacked)
    return jnp.fft.fft(jnp.concatenate([values, jnp.zeros_like(values)], axis=0), axis=0)


def spectrum_screen(stacked):
    values = as_complex(stacked)
    middle = NE // 2
    padded = jnp.concatenate([values[middle:], jnp.zeros_like(values), values[:middle]], axis=0)
    return jnp.fft.fft(padded, axis=0)


def back_to_energy(spectrum):
    values = jnp.fft.ifft(spectrum, axis=0)[:NE]
    return jnp.stack([jnp.real(values), jnp.imag(values)], axis=1).astype(jnp.bfloat16)


def reference(green_lesser, screened_lesser, green_retarded, screened_retarded, left_green, coupling):
    def convolve_slab(slab_index):
        def pick(array):
            return lax.dynamic_index_in_dim(array, slab_index, axis=1, keepdims=False)

        green_less = spectrum_green(pick(green_lesser))
        green_ret = spectrum_green(pick(green_retarded))
        screen_less = spectrum_screen(pick(screened_lesser))
        screen_ret = spectrum_screen(pick(screened_retarded))
        lesser_hat = green_less * screen_less
        retarded_hat = green_ret * screen_less + green_less * screen_ret + green_ret * screen_ret
        return back_to_energy(lesser_hat), back_to_energy(retarded_hat)

    slab_numbers = jnp.arange(NSLAB, dtype=jnp.int32)
    sigma_lesser, sigma_ret = lax.map(convolve_slab, slab_numbers)

    def slab_step(state, slab_index):
        green_slab = lax.dynamic_index_in_dim(left_green, slab_index, axis=1, keepdims=False).astype(jnp.float32)
        coupling_slab = lax.dynamic_index_in_dim(coupling, slab_index, axis=0, keepdims=False).astype(jnp.float32)
        sigma_slab = lax.dynamic_index_in_dim(sigma_lesser, slab_index, axis=0, keepdims=False).astype(jnp.float32)
        propagator = rounded(complex_product("nij,jk->nik", green_slab, coupling_slab)).astype(jnp.float32)
        half_source = rounded(complex_product("nij,njk->nik", green_slab, sigma_slab)).astype(jnp.float32)
        source = adjoint_product("nij,nkj->nik", half_source, green_slab)
        inner = complex_product("nij,njk->nik", propagator, state)
        new_state = source + adjoint_product("nij,nkj->nik", inner, propagator)
        return new_state, new_state.astype(jnp.bfloat16)

    initial = jnp.zeros((NE, 2, B, B), jnp.float32)
    _, lesser_left = lax.scan(slab_step, initial, slab_numbers)
    return jnp.moveaxis(lesser_left, 0, 1), jnp.moveaxis(sigma_ret, 0, 1)
```

```python
import functools

import jax
import jax.numpy as jnp
from jax import lax
from jax.experimental import pallas as pl
from jax.experimental.pallas import tpu as pltpu
from jax.sharding import PartitionSpec as P

VMEM = pl.BlockSpec(memory_space=pltpu.VMEM)
F32, BF16 = jnp.float32, jnp.bfloat16


def call(kernel, outs, args, flops, name):
    moved = sum(a.size * a.dtype.itemsize for a in args)
    moved += sum(o.size * o.dtype.itemsize for o in outs)
    return pl.pallas_call(
        kernel,
        out_shape=outs,
        in_specs=[VMEM] * len(args),
        out_specs=[VMEM] * len(outs),
        cost_estimate=pl.CostEstimate(flops=flops, bytes_accessed=moved, transcendentals=0),
        name=name,
    )(*args)


def shaped(shape, dtype):
    return jax.ShapeDtypeStruct(shape, dtype)


def pack_kernel(first, second, out):
    parts, _, _, rows, columns = out.shape
    for position, source in enumerate((first, second)):
        for entry in range(2):
            out[:, position, entry] = source[entry].reshape(parts, rows, columns)


def pack(first, second, parts):
    _, order, columns = first.shape
    out = shaped((parts, 2, 2, order // parts, columns), first.dtype)
    return call(pack_kernel, [out], [first, second], 0, "pack")[0]


def real_convolution(first, second, energies):
    middle = energies // 2
    sums = []
    for n in range(energies):
        total = None
        for m in range(energies):
            lag = n - m + middle
            if 0 <= lag < energies:
                term = first[m] * second[lag]
                total = term if total is None else total + term
        sums.append(total)
    return sums


def complex_convolution(load_first, load_second, store, energies):
    if energies <= 16:
        span = range(energies)
        both = real_convolution(
            [load_first(m, 0) + load_first(m, 1) for m in span],
            [load_second(j, 0) for j in span],
            energies,
        )
        cross = real_convolution(
            [load_first(m, 0) for m in span],
            [load_second(j, 1) - load_second(j, 0) for j in span],
            energies,
        )
        other = real_convolution(
            [load_first(m, 1) for m in span],
            [load_second(j, 0) + load_second(j, 1) for j in span],
            energies,
        )
        for n in span:
            store(n, both[n] - other[n], both[n] + cross[n])
        return
    middle = energies // 2

    def one_energy(n, carry):
        def one_term(m, sums):
            lag = n - m + middle
            a, b = load_first(m, 0), load_first(m, 1)
            c, d = load_second(lag, 0), load_second(lag, 1)
            return (sums[0] + (a * c - b * d), sums[1] + (a * d + b * c))

        zero = jnp.zeros(load_first(0, 0).shape, F32)
        low = jnp.maximum(n + middle - energies + 1, 0)
        high = jnp.minimum(n + middle, energies - 1) + 1
        real, imag = lax.fori_loop(low, high, one_term, (zero, zero))
        store(n, real, imag)
        return carry

    lax.fori_loop(0, energies, one_energy, 0)


def tiles(rows, columns):
    high = 8 if rows % 8 == 0 else rows
    wide = 128 if columns % 128 == 0 else columns
    return high, wide, columns // wide, (rows // high) * (columns // wide)


def each_tile(rows, columns, work):
    high, wide, across, count = tiles(rows, columns)

    def step(i, carry):
        row = pl.multiple_of((i // across) * high, high)
        column = pl.multiple_of((i % across) * wide, wide)
        work(pl.ds(row, high), pl.ds(column, wide))
        return carry

    lax.fori_loop(0, count, step, 0)


def lesser_kernel(data, out, exact):
    energies, _, rows, columns = out.shape

    def work(r, c):
        def store(n, real, imag):
            for entry, value in enumerate((real, imag)):
                exact[n, entry, r, c] = value
                out[n, entry, r, c] = value.astype(out.dtype)

        complex_convolution(
            lambda m, entry: data[m, 0, entry, r, c].astype(F32),
            lambda j, entry: data[j, 1, entry, r, c].astype(F32),
            store,
            energies,
        )

    each_tile(rows, columns, work)


def retarded_kernel(lesser, retarded, exact, out):
    energies, _, rows, columns = out.shape

    def work(r, c):
        def both(index, which, entry):
            left = lesser[index, which, entry, r, c].astype(F32)
            return left + retarded[index, which, entry, r, c].astype(F32)

        def store(n, real, imag):
            for entry, value in enumerate((real, imag)):
                out[n, entry, r, c] = (value - exact[n, entry, r, c]).astype(out.dtype)

        complex_convolution(
            lambda m, entry: both(m, 0, entry),
            lambda j, entry: both(j, 1, entry),
            store,
            energies,
        )

    each_tile(rows, columns, work)


def lesser_convolution(data):
    energies, _, _, rows, columns = data.shape
    shape = (energies, 2, rows, columns)
    flops = 9 * energies * energies * rows * columns
    return call(lesser_kernel, [shaped(shape, BF16), shaped(shape, F32)], [data], flops, "lesser")


def retarded_convolution(lesser, retarded, exact):
    energies, _, _, rows, columns = lesser.shape
    flops = 9 * energies * energies * rows * columns
    out = shaped((energies, 2, rows, columns), BF16)
    return call(retarded_kernel, [out], [lesser, retarded, exact], flops, "retarded")[0]


def dot(first, second):
    return lax.dot_general(first, second, (((1,), (0,)), ((), ())), preferred_element_type=F32)


def dot_t(first, second):
    return lax.dot_general(first, second, (((1,), (1,)), ((), ())), preferred_element_type=F32)


def product(a, b, c, d):
    return dot(a, c) - dot(b, d), dot(a, d) + dot(b, c)


def adjoint(a, b, c, d):
    return dot_t(a, c) + dot_t(b, d), dot_t(b, c) - dot_t(a, d)


def propagator_kernel(left, coupling, out):
    real, imag = product(left[0], left[1], coupling[0], coupling[1])
    out[0] = real.astype(out.dtype)
    out[1] = imag.astype(out.dtype)


def source_kernel(left, sigma, out, sent):
    order = left.shape[1]
    s_real = sigma[:, 0].reshape(order, order)
    s_imag = sigma[:, 1].reshape(order, order)
    real, imag = product(left[0], left[1], s_real, s_imag)
    real, imag = adjoint(real.astype(BF16), imag.astype(BF16), left[0], left[1])
    out[0] = real
    out[1] = imag
    sent[0] = real.astype(sent.dtype)
    sent[1] = imag.astype(sent.dtype)


def split(values):
    upper = values.astype(BF16)
    return upper, (values - upper.astype(F32)).astype(BF16)


def state_kernel(source, propagator, entering, out):
    p_real, p_imag = propagator[0], propagator[1]
    real, imag = product(p_real, p_imag, entering[0], entering[1])
    (real, real_low), (imag, imag_low) = split(real), split(imag)
    new_real, new_imag = adjoint(real, imag, p_real, p_imag)
    low_real, low_imag = adjoint(real_low, imag_low, p_real, p_imag)
    out[0] = (source[0] + (new_real + low_real)).astype(out.dtype)
    out[1] = (source[1] + (new_imag + low_imag)).astype(out.dtype)


def unpack_kernel(sigma, out):
    order = out.shape[1]
    for entry in range(2):
        out[entry] = sigma[:, entry].reshape(order, order)


def body(green_lesser, screened_lesser, green_retarded, screened_retarded, left_green, coupling):
    block = green_lesser.shape[2:]
    order = block[-1]
    assert green_lesser.shape[:2] == (1, 1) and coupling.shape[0] == 1
    parts = lax.axis_size("energy")
    exchange = functools.partial(
        lax.all_to_all, axis_name="energy", split_axis=0, concat_axis=0, tiled=True
    )
    green_l, screen_l = green_lesser.reshape(block), screened_lesser.reshape(block)
    green_r, screen_r = green_retarded.reshape(block), screened_retarded.reshape(block)
    left, hop = left_green.reshape(block), coupling.reshape(block)
    cube = 8 * order**3

    lesser = exchange(pack(green_l, screen_l, parts))
    retarded = exchange(pack(green_r, screen_r, parts))
    sigma_lesser, exact = lesser_convolution(lesser)
    sigma_lesser = exchange(sigma_lesser)
    sigma_retarded = exchange(retarded_convolution(lesser, retarded, exact))

    propagator = call(propagator_kernel, [shaped(block, BF16)], [left, hop], cube, "propagator")[0]
    source, state = call(
        source_kernel,
        [shaped(block, F32), shaped(block, BF16)],
        [left, sigma_lesser],
        2 * cube,
        "source",
    )
    devices = lax.axis_size("space")
    pairs = [(i, i + 1) for i in range(devices - 1)]
    for _ in range(devices - 1):
        entering = lax.ppermute(state, "space", pairs)
        state = call(
            state_kernel, [shaped(block, BF16)], [source, propagator, entering], 3 * cube, "state"
        )[0]
    retarded_out = call(unpack_kernel, [shaped(block, BF16)], [sigma_retarded], 0, "unpack")[0]
    return state.reshape(left_green.shape), retarded_out.reshape(left_green.shape)


def solution(mesh):
    split_spec = P("energy", "space", None, None, None)
    return jax.shard_map(
        body,
        mesh=mesh,
        in_specs=(split_spec,) * 5 + (P("space", None, None, None),),
        out_specs=(split_spec, split_spec),
        check_vma=False,
    )
```

```python
import functools

import jax
import jax.numpy as jnp
from jax import lax
from jax.experimental import pallas as pl
from jax.experimental.pallas import tpu as pltpu
from jax.sharding import PartitionSpec as P

VMEM = pl.BlockSpec(memory_space=pltpu.VMEM)
F32, BF16 = jnp.float32, jnp.bfloat16


def on_chip(array):
    return pltpu.with_memory_space_constraint(array, pltpu.VMEM)


def call(kernel, outs, args, flops, name, on_chip_out=()):
    moved = sum(a.size * a.dtype.itemsize for a in args)
    moved += sum(o.size * o.dtype.itemsize for o in outs)
    return pl.pallas_call(
        kernel,
        out_shape=[
            pltpu.VMEM(o.shape, o.dtype) if i in on_chip_out else o for i, o in enumerate(outs)
        ],
        in_specs=[VMEM] * len(args),
        out_specs=[VMEM] * len(outs),
        cost_estimate=pl.CostEstimate(flops=flops, bytes_accessed=moved, transcendentals=0),
        name=name,
    )(*args)


def shaped(shape, dtype):
    return jax.ShapeDtypeStruct(shape, dtype)


def pack_kernel(first, second, out):
    parts, _, _, rows, columns = out.shape
    for position, source in enumerate((first, second)):
        for entry in range(2):
            out[:, position, entry] = source[entry].reshape(parts, rows, columns)


def pack(first, second, parts):
    _, order, columns = first.shape
    out = shaped((parts, 2, 2, order // parts, columns), first.dtype)
    return call(pack_kernel, [out], [first, second], 0, "pack", (0,))[0]


def real_convolution(first, second, energies):
    middle = energies // 2
    sums = []
    for n in range(energies):
        total = None
        for m in range(energies):
            lag = n - m + middle
            if 0 <= lag < energies:
                term = first[m] * second[lag]
                total = term if total is None else total + term
        sums.append(total)
    return sums


def complex_convolution(load_first, load_second, store, energies):
    if energies <= 16:
        span = range(energies)
        both = real_convolution(
            [load_first(m, 0) + load_first(m, 1) for m in span],
            [load_second(j, 0) for j in span],
            energies,
        )
        cross = real_convolution(
            [load_first(m, 0) for m in span],
            [load_second(j, 1) - load_second(j, 0) for j in span],
            energies,
        )
        other = real_convolution(
            [load_first(m, 1) for m in span],
            [load_second(j, 0) + load_second(j, 1) for j in span],
            energies,
        )
        for n in span:
            store(n, both[n] - other[n], both[n] + cross[n])
        return
    middle = energies // 2

    def one_energy(n, carry):
        def one_term(m, sums):
            lag = n - m + middle
            a, b = load_first(m, 0), load_first(m, 1)
            c, d = load_second(lag, 0), load_second(lag, 1)
            return (sums[0] + (a * c - b * d), sums[1] + (a * d + b * c))

        zero = jnp.zeros(load_first(0, 0).shape, F32)
        low = jnp.maximum(n + middle - energies + 1, 0)
        high = jnp.minimum(n + middle, energies - 1) + 1
        real, imag = lax.fori_loop(low, high, one_term, (zero, zero))
        store(n, real, imag)
        return carry

    lax.fori_loop(0, energies, one_energy, 0)


def tiles(rows, columns):
    high = 8 if rows % 8 == 0 else rows
    wide = 128 if columns % 128 == 0 else columns
    return high, wide, columns // wide, (rows // high) * (columns // wide)


def each_tile(rows, columns, work):
    high, wide, across, count = tiles(rows, columns)

    def step(i, carry):
        row = pl.multiple_of((i // across) * high, high)
        column = pl.multiple_of((i % across) * wide, wide)
        work(pl.ds(row, high), pl.ds(column, wide))
        return carry

    lax.fori_loop(0, count, step, 0)


def lesser_kernel(data, out, exact):
    energies, _, rows, columns = out.shape

    def work(r, c):
        def store(n, real, imag):
            for entry, value in enumerate((real, imag)):
                exact[n, entry, r, c] = value
                out[n, entry, r, c] = value.astype(out.dtype)

        complex_convolution(
            lambda m, entry: data[m, 0, entry, r, c].astype(F32),
            lambda j, entry: data[j, 1, entry, r, c].astype(F32),
            store,
            energies,
        )

    each_tile(rows, columns, work)


def retarded_kernel(lesser, retarded, exact, out):
    energies, _, rows, columns = out.shape

    def work(r, c):
        def both(index, which, entry):
            left = lesser[index, which, entry, r, c].astype(F32)
            return left + retarded[index, which, entry, r, c].astype(F32)

        def store(n, real, imag):
            for entry, value in enumerate((real, imag)):
                out[n, entry, r, c] = (value - exact[n, entry, r, c]).astype(out.dtype)

        complex_convolution(
            lambda m, entry: both(m, 0, entry),
            lambda j, entry: both(j, 1, entry),
            store,
            energies,
        )

    each_tile(rows, columns, work)


def lesser_convolution(data):
    energies, _, _, rows, columns = data.shape
    shape = (energies, 2, rows, columns)
    flops = 9 * energies * energies * rows * columns
    return call(lesser_kernel, [shaped(shape, BF16), shaped(shape, F32)], [on_chip(data)], flops, "lesser", (0, 1))


def retarded_convolution(lesser, retarded, exact):
    energies, _, _, rows, columns = lesser.shape
    flops = 9 * energies * energies * rows * columns
    out = shaped((energies, 2, rows, columns), BF16)
    return call(retarded_kernel, [out], [on_chip(lesser), on_chip(retarded), on_chip(exact)], flops, "retarded", (0,))[0]


def dot(first, second):
    return lax.dot_general(first, second, (((1,), (0,)), ((), ())), preferred_element_type=F32)


def dot_t(first, second):
    return lax.dot_general(first, second, (((1,), (1,)), ((), ())), preferred_element_type=F32)


def product(a, b, c, d):
    return dot(a, c) - dot(b, d), dot(a, d) + dot(b, c)


def adjoint(a, b, c, d):
    return dot_t(a, c) + dot_t(b, d), dot_t(b, c) - dot_t(a, d)


def propagator_kernel(left, coupling, out):
    real, imag = product(left[0], left[1], coupling[0], coupling[1])
    out[0] = real.astype(out.dtype)
    out[1] = imag.astype(out.dtype)


def source_kernel(left, sigma, out, sent):
    order = left.shape[1]
    s_real = sigma[:, 0].reshape(order, order)
    s_imag = sigma[:, 1].reshape(order, order)
    real, imag = product(left[0], left[1], s_real, s_imag)
    real, imag = adjoint(real.astype(BF16), imag.astype(BF16), left[0], left[1])
    out[0] = real
    out[1] = imag
    sent[0] = real.astype(sent.dtype)
    sent[1] = imag.astype(sent.dtype)


def split(values):
    upper = values.astype(BF16)
    return upper, (values - upper.astype(F32)).astype(BF16)


def state_kernel(source, propagator, entering, out):
    p_real, p_imag = propagator[0], propagator[1]
    real, imag = product(p_real, p_imag, entering[0], entering[1])
    (real, real_low), (imag, imag_low) = split(real), split(imag)
    new_real, new_imag = adjoint(real, imag, p_real, p_imag)
    low_real, low_imag = adjoint(real_low, imag_low, p_real, p_imag)
    out[0] = (source[0] + (new_real + low_real)).astype(out.dtype)
    out[1] = (source[1] + (new_imag + low_imag)).astype(out.dtype)


def unpack_kernel(sigma, out):
    order = out.shape[1]
    for entry in range(2):
        out[entry] = sigma[:, entry].reshape(order, order)


def body(green_lesser, screened_lesser, green_retarded, screened_retarded, left_green, coupling):
    block = green_lesser.shape[2:]
    order = block[-1]
    assert green_lesser.shape[:2] == (1, 1) and coupling.shape[0] == 1
    parts = lax.axis_size("energy")
    exchange = functools.partial(
        lax.all_to_all, axis_name="energy", split_axis=0, concat_axis=0, tiled=True
    )
    green_l, screen_l = green_lesser.reshape(block), screened_lesser.reshape(block)
    green_r, screen_r = green_retarded.reshape(block), screened_retarded.reshape(block)
    left, hop = left_green.reshape(block), coupling.reshape(block)
    cube = 8 * order**3

    merged = exchange(jnp.concatenate([pack(green_l, screen_l, parts), pack(green_r, screen_r, parts)], axis=1))
    lesser, retarded = merged[:, :2], merged[:, 2:]
    sigma_lesser, exact = lesser_convolution(lesser)
    sigma_lesser = exchange(sigma_lesser)
    sigma_retarded = exchange(retarded_convolution(lesser, retarded, exact))

    propagator = call(propagator_kernel, [shaped(block, BF16)], [left, hop], cube, "propagator", (0,))[0]
    source, state = call(
        source_kernel,
        [shaped(block, F32), shaped(block, BF16)],
        [left, on_chip(sigma_lesser)],
        2 * cube,
        "source",
        (0, 1),
    )
    devices = lax.axis_size("space")
    pairs = [(i, i + 1) for i in range(devices - 1)]
    for _ in range(devices - 1):
        entering = lax.ppermute(state, "space", pairs)
        state = call(
            state_kernel, [shaped(block, BF16)], [on_chip(source), on_chip(propagator), on_chip(entering)], 3 * cube, "state"
        )[0]
    retarded_out = call(unpack_kernel, [shaped(block, BF16)], [on_chip(sigma_retarded)], 0, "unpack")[0]
    return state.reshape(left_green.shape), retarded_out.reshape(left_green.shape)


def solution(mesh):
    split_spec = P("energy", "space", None, None, None)
    return jax.shard_map(
        body,
        mesh=mesh,
        in_specs=(split_spec,) * 5 + (P("space", None, None, None),),
        out_specs=(split_spec, split_spec),
        check_vma=False,
    )
```

```python
import functools

import jax
import jax.numpy as jnp
from jax import lax
from jax.experimental import pallas as pl
from jax.experimental.pallas import tpu as pltpu
from jax.sharding import PartitionSpec as P

VMEM = pl.BlockSpec(memory_space=pltpu.VMEM)
F32, BF16 = jnp.float32, jnp.bfloat16


def on_chip(array):
    return pltpu.with_memory_space_constraint(array, pltpu.VMEM)


def call(kernel, outs, args, flops, on_chip_out=()):
    moved = sum(a.size * a.dtype.itemsize for a in args)
    moved += sum(o.size * o.dtype.itemsize for o in outs)
    return pl.pallas_call(
        kernel,
        out_shape=[
            pltpu.VMEM(o.shape, o.dtype) if i in on_chip_out else o for i, o in enumerate(outs)
        ],
        in_specs=[VMEM] * len(args),
        out_specs=[VMEM] * len(outs),
        cost_estimate=pl.CostEstimate(flops=flops, bytes_accessed=moved, transcendentals=0),
    )(*args)


def shaped(shape, dtype):
    return jax.ShapeDtypeStruct(shape, dtype)


def pack_kernel(first, second, out):
    parts, _, _, rows, columns = out.shape
    for position, source in enumerate((first, second)):
        for entry in range(2):
            out[:, position, entry] = source[entry].reshape(parts, rows, columns)


def pack(first, second, parts):
    _, order, columns = first.shape
    out = shaped((parts, 2, 2, order // parts, columns), first.dtype)
    return call(pack_kernel, [out], [first, second], 0, (0,))[0]


def real_convolution(first, second, energies):
    middle = energies // 2
    sums = []
    for n in range(energies):
        total = None
        for m in range(energies):
            lag = n - m + middle
            if 0 <= lag < energies:
                term = first[m] * second[lag]
                total = term if total is None else total + term
        sums.append(total)
    return sums


def complex_convolution(load_first, load_second, store, energies):
    if energies <= 16:
        span = range(energies)
        both = real_convolution(
            [load_first(m, 0) + load_first(m, 1) for m in span],
            [load_second(j, 0) for j in span],
            energies,
        )
        cross = real_convolution(
            [load_first(m, 0) for m in span],
            [load_second(j, 1) - load_second(j, 0) for j in span],
            energies,
        )
        other = real_convolution(
            [load_first(m, 1) for m in span],
            [load_second(j, 0) + load_second(j, 1) for j in span],
            energies,
        )
        for n in span:
            store(n, both[n] - other[n], both[n] + cross[n])
        return
    middle = energies // 2

    def one_energy(n, carry):
        def one_term(m, sums):
            lag = n - m + middle
            a, b = load_first(m, 0), load_first(m, 1)
            c, d = load_second(lag, 0), load_second(lag, 1)
            return (sums[0] + (a * c - b * d), sums[1] + (a * d + b * c))

        zero = jnp.zeros(load_first(0, 0).shape, F32)
        low = jnp.maximum(n + middle - energies + 1, 0)
        high = jnp.minimum(n + middle, energies - 1) + 1
        real, imag = lax.fori_loop(low, high, one_term, (zero, zero))
        store(n, real, imag)
        return carry

    lax.fori_loop(0, energies, one_energy, 0)


def tiles(rows, columns):
    high = 8 if rows % 8 == 0 else rows
    wide = 128 if columns % 128 == 0 else columns
    return high, wide, columns // wide, (rows // high) * (columns // wide)


def each_tile(rows, columns, work):
    high, wide, across, count = tiles(rows, columns)

    def step(i, carry):
        row = pl.multiple_of((i // across) * high, high)
        column = pl.multiple_of((i % across) * wide, wide)
        work(pl.ds(row, high), pl.ds(column, wide))
        return carry

    lax.fori_loop(0, count, step, 0)


def lesser_kernel(data, out, exact):
    energies, _, rows, columns = out.shape

    def work(r, c):
        def store(n, real, imag):
            for entry, value in enumerate((real, imag)):
                exact[n, entry, r, c] = value
                out[n, entry, r, c] = value.astype(out.dtype)

        complex_convolution(
            lambda m, entry: data[m, 0, entry, r, c].astype(F32),
            lambda j, entry: data[j, 1, entry, r, c].astype(F32),
            store,
            energies,
        )

    each_tile(rows, columns, work)


def combine(lesser, retarded, exact, out):
    energies, _, rows, columns = out.shape

    def work(r, c):
        def both(index, which, entry):
            left = lesser[index, which, entry, r, c].astype(F32)
            return left + retarded[index, which, entry, r, c].astype(F32)

        def store(n, real, imag):
            for entry, value in enumerate((real, imag)):
                out[n, entry, r, c] = (value - exact[n, entry, r, c]).astype(out.dtype)

        complex_convolution(
            lambda m, entry: both(m, 0, entry),
            lambda j, entry: both(j, 1, entry),
            store,
            energies,
        )

    each_tile(rows, columns, work)


def lesser_convolution(data):
    energies, _, _, rows, columns = data.shape
    shape = (energies, 2, rows, columns)
    flops = 9 * energies * energies * rows * columns
    return call(lesser_kernel, [shaped(shape, BF16), shaped(shape, F32)], [on_chip(data)], flops, (0, 1))


def retarded_convolution(lesser, retarded, exact):
    energies, _, _, rows, columns = lesser.shape
    flops = 9 * energies * energies * rows * columns
    out = shaped((energies, 2, rows, columns), BF16)
    args = [on_chip(lesser), on_chip(retarded), on_chip(exact)]
    return call(combine, [out], args, flops, (0,))[0]


class Stages:
    def __init__(self, parts, inner):
        self.parts, self.inner, self.outer = parts, inner, parts // inner

    def here(self):
        me = lax.axis_index("energy")
        return lax.div(me, self.inner), lax.rem(me, self.inner)

    def place(self, me, t, s):
        return (me[0] ^ t) * self.inner + (me[1] ^ s)

    def permute(self, array, step):
        pairs = [(i, i ^ step) for i in range(self.parts)]
        return lax.ppermute(array, "energy", pairs)

    def within(self, arrays):
        return [self.permute(a, s) for s, a in enumerate(arrays, 1)]

    def across(self, arrays):
        sent = [self.permute(a, t * self.inner) for t, a in enumerate(arrays) if t]
        return [arrays[0], *sent]

    def call(self, kernel, outs, args, flops, scratch=(), on_chip_out=True):
        moved = sum(a.size * a.dtype.itemsize for a in args)
        moved += sum(o.size * o.dtype.itemsize for o in outs)
        return pl.pallas_call(
            functools.partial(kernel, self),
            out_shape=[pltpu.VMEM(o.shape, o.dtype) if on_chip_out else o for o in outs],
            in_specs=[VMEM] * len(args),
            out_specs=[VMEM] * len(outs),
            scratch_shapes=scratch,
            cost_estimate=pl.CostEstimate(
                flops=flops, bytes_accessed=moved, transcendentals=0
            ),
        )(*args)


def rows_at(index, rows):
    return pl.ds(pl.multiple_of(index * rows, rows), rows)


def spread_kernel(stages, first, second, *outs):
    me = stages.here()
    rows = outs[0].shape[3]
    for s, out in enumerate(outs, 1):
        for o in range(stages.outer):
            at = rows_at(o * stages.inner + (me[1] ^ s), rows)
            for position, source in enumerate((first, second)):
                for entry in range(2):
                    out[o, position, entry] = source[entry, at, :]


def gather_kernel(stages, first, second, *refs):
    me = stages.here()
    received, outs = refs[: stages.inner - 1], refs[stages.inner - 1 :]
    rows = outs[0].shape[3]
    for t, out in enumerate(outs):
        at = rows_at(stages.place(me, t, 0), rows)
        for position, source in enumerate((first, second)):
            for entry in range(2):
                out[0, position, entry] = source[entry, at, :]
        for s, piece in enumerate(received, 1):
            out[s] = piece[me[0] ^ t]


def staged_in(stages, first, second):
    _, order, columns = first.shape
    block = (2, 2, order // stages.parts, columns)
    pieces = []
    if stages.inner > 1:
        outs = [shaped((stages.outer, *block), BF16)] * (stages.inner - 1)
        pieces = stages.call(spread_kernel, outs, [first, second], 0)
        pieces = stages.within(pieces)
    outs = [shaped((stages.inner, *block), BF16)] * stages.outer
    args = [first, second, *map(on_chip, pieces)]
    return stages.across(stages.call(gather_kernel, outs, args, 0))


def spread_lesser_kernel(stages, *refs):
    pieces, (data, out, exact, *spread) = refs[: stages.outer], refs[stages.outer :]
    me = stages.here()
    for t, piece in enumerate(pieces):
        for s in range(stages.inner):
            data[stages.place(me, t, s)] = piece[s]
    lesser_kernel(data, out, exact)
    for s, other in enumerate(spread, 1):
        for o in range(stages.outer):
            other[o] = out[o * stages.inner + (me[1] ^ s)]


def regroup_kernel(stages, sigma, *refs):
    me = stages.here()
    received, outs = refs[: stages.inner - 1], refs[stages.inner - 1 :]
    for t, out in enumerate(outs):
        out[0] = sigma[stages.place(me, t, 0)]
        for s, piece in enumerate(received, 1):
            out[s] = piece[me[0] ^ t]


def staged_lesser(stages, pieces):
    _, _, _, rows, columns = pieces[0].shape
    energies = stages.parts
    flops = 9 * energies * energies * rows * columns
    tile = (2, rows, columns)
    outs = [shaped((energies, 2, *tile), BF16)]
    outs += [shaped((energies, *tile), BF16), shaped((energies, *tile), F32)]
    outs += [shaped((stages.outer, *tile), BF16)] * (stages.inner - 1)
    lesser, sigma, exact, *spread = stages.call(
        spread_lesser_kernel, outs, [on_chip(p) for p in pieces], flops
    )
    spread = stages.within(spread)
    outs = [shaped((stages.inner, *tile), BF16)] * stages.outer
    args = [on_chip(a) for a in (sigma, *spread)]
    pieces = stages.across(stages.call(regroup_kernel, outs, args, 0))
    return lesser, pieces, exact


def placed(stages, pieces, out):
    me = stages.here()
    rows = pieces[0].shape[2]
    for t, piece in enumerate(pieces):
        for s in range(stages.inner):
            at = rows_at(stages.place(me, t, s), rows)
            for entry in range(2):
                out[entry, at, :] = piece[s, entry]


def dot(first, second):
    return lax.dot_general(first, second, (((1,), (0,)), ((), ())), preferred_element_type=F32)


def dot_t(first, second):
    return lax.dot_general(first, second, (((1,), (1,)), ((), ())), preferred_element_type=F32)


def product(a, b, c, d):
    return dot(a, c) - dot(b, d), dot(a, d) + dot(b, c)


def adjoint(a, b, c, d):
    return dot_t(a, c) + dot_t(b, d), dot_t(b, c) - dot_t(a, d)


def propagator_real(left, coupling, out):
    out[...] = (dot(left[0], coupling[0]) - dot(left[1], coupling[1])).astype(out.dtype)


def propagator_imag(left, coupling, out):
    out[...] = (dot(left[0], coupling[1]) + dot(left[1], coupling[0])).astype(out.dtype)


def write_source(left, s_real, s_imag, out, sent):
    real, imag = product(left[0], left[1], s_real, s_imag)
    real, imag = adjoint(real.astype(BF16), imag.astype(BF16), left[0], left[1])
    out[0] = real
    out[1] = imag
    sent[0] = real.astype(sent.dtype)
    sent[1] = imag.astype(sent.dtype)


def source_kernel(left, sigma, out, sent):
    order = left.shape[1]
    s_real = sigma[:, 0].reshape(order, order)
    s_imag = sigma[:, 1].reshape(order, order)
    write_source(left, s_real, s_imag, out, sent)


def staged_source_kernel(stages, left, *refs):
    *pieces, out, sent, sigma = refs
    placed(stages, pieces, sigma)
    write_source(left, sigma[0], sigma[1], out, sent)


def split(values):
    upper = values.astype(BF16)
    return upper, (values - upper.astype(F32)).astype(BF16)


def state_kernel(source, p_real, p_imag, entering, out):
    p_real, p_imag = p_real[...], p_imag[...]
    enters = lax.axis_index("space") > 0
    arrived = [jnp.where(enters, entering[i], jnp.zeros_like(entering[i])) for i in range(2)]
    real, imag = product(p_real, p_imag, *arrived)
    (real, real_low), (imag, imag_low) = split(real), split(imag)
    new_real, new_imag = adjoint(real, imag, p_real, p_imag)
    low_real, low_imag = adjoint(real_low, imag_low, p_real, p_imag)
    out[0] = (source[0] + (new_real + low_real)).astype(out.dtype)
    out[1] = (source[1] + (new_imag + low_imag)).astype(out.dtype)


def unpack_kernel(sigma, out):
    order = out.shape[1]
    for entry in range(2):
        out[entry] = sigma[:, entry].reshape(order, order)


INNER = 2


def body(green_lesser, screened_lesser, green_retarded, screened_retarded, left_green, coupling):
    block = green_lesser.shape[2:]
    order = block[-1]
    assert green_lesser.shape[:2] == (1, 1) and coupling.shape[0] == 1
    parts = lax.axis_size("energy")

    def exchange(array):
        return lax.all_to_all(array, "energy", split_axis=0, concat_axis=0, tiled=True)

    green_l, screen_l = green_lesser.reshape(block), screened_lesser.reshape(block)
    green_r, screen_r = green_retarded.reshape(block), screened_retarded.reshape(block)
    left, hop = left_green.reshape(block), coupling.reshape(block)
    cube = 8 * order**3
    staged = parts & (parts - 1) == 0 and order // parts % 8 == 0

    if staged:
        stages = Stages(parts, INNER)
        pieces = staged_in(stages, green_l, screen_l)
        lesser, sigma_lesser, exact = staged_lesser(stages, pieces)
    else:
        lesser = exchange(pack(green_l, screen_l, parts))
        sigma_lesser, exact = lesser_convolution(lesser)
        sigma_lesser = exchange(sigma_lesser)
    packed = pack(green_r, screen_r, parts)
    retarded = exchange(packed)
    sigma_retarded = retarded_convolution(lesser, retarded, exact)
    args = [on_chip(exchange(sigma_retarded))]
    retarded_out = call(unpack_kernel, [shaped(block, BF16)], args, 0)[0]

    propagator = []
    for kernel in (propagator_real, propagator_imag):
        out = [shaped(block[1:], BF16)]
        propagator += call(kernel, out, [left, hop], cube // 2, (0,))
    outs = [shaped(block, F32), shaped(block, BF16)]
    if staged:
        args = [left, *map(on_chip, sigma_lesser)]
        scratch = [pltpu.VMEM(block, BF16)]
        source, state = stages.call(staged_source_kernel, outs, args, 2 * cube, scratch)
    else:
        args = [left, on_chip(sigma_lesser)]
        source, state = call(source_kernel, outs, args, 2 * cube, (0, 1))
    devices = lax.axis_size("space")
    pairs = [(i, (i + 1) % devices) for i in range(devices)]
    for _ in range(devices - 1):
        entering = lax.ppermute(state, "space", pairs)
        state = call(
            state_kernel,
            [shaped(block, BF16)],
            [on_chip(a) for a in (source, *propagator, entering)],
            3 * cube,
        )[0]
    return state.reshape(left_green.shape), retarded_out.reshape(left_green.shape)


def solution(mesh):
    split_spec = P("energy", "space", None, None, None)
    return jax.shard_map(
        body,
        mesh=mesh,
        in_specs=(split_spec,) * 5 + (P("space", None, None, None),),
        out_specs=(split_spec, split_spec),
        check_vma=False,
    )
```
